32 devices in a mesh: ctx: 8 (over z, y), head: 4 (over x, core).
Axes of the slice: x: 2, y: 2, z: 4, core: 2. Of those that a mesh axis runs over, the one named last changes fastest.
Arguments:
- x_in: bfloat16 [4096, 1024], P(('ctx', 'head')), may hold values from -6 to 6
- in_weight: bfloat16 [1024, 4120], P(('ctx', 'head')), may hold values from -1 to 1
- out_weight: bfloat16 [2048, 1024], P(('ctx', 'head')), may hold values from -0.1875 to 0.1875
- gu_weight: bfloat16 [1024, 4096], P(('ctx', 'head')), may hold values from -0.1875 to 0.1875
- down_weight: bfloat16 [2048, 1024], P(('ctx', 'head')), may hold values from -0.125 to 0.125
- norm_gain: bfloat16 [1024], P(('ctx', 'head')), may hold values from 0.5 to 1.5
- mixer_gain: bfloat16 [1536], P(('ctx', 'head')), may hold values from 0.5 to 1.5
- ffn_gain: bfloat16 [1024], P(('ctx', 'head')), may hold values from 0.5 to 1.5
- conv_weight: bfloat16 [1792, 4], P(('ctx', 'head')), may hold values from -3 to 3
- conv_bias: bfloat16 [1792], P(('ctx', 'head')), may hold values from -3 to 3
- dt_bias: float32 [24], P('head'), may hold values from -1 to 1
- a_log: float32 [24], P('head'), may hold values from -14 to -2
- skip_gain: float32 [24], P('head'), may hold values from 0 to 2
- out_grad: bfloat16 [4096, 1024], P(('ctx', 'head')), may hold values from -6 to 6
Outputs:
- y_out: bfloat16 [4096, 1024], P(('ctx', 'head'))
- x_grad: float32 [4096, 1024], P(('ctx', 'head'))
- in_weight_grad: float32 [1024, 4120], P(('ctx', 'head'))
- out_weight_grad: float32 [2048, 1024], P(('ctx', 'head'))
- gu_weight_grad: float32 [1024, 4096], P(('ctx', 'head'))
- down_weight_grad: float32 [2048, 1024], P(('ctx', 'head'))
- norm_gain_grad: float32 [1024], P(('ctx', 'head'))
- mixer_gain_grad: float32 [1536], P(('ctx', 'head'))
- ffn_gain_grad: float32 [1024], P(('ctx', 'head'))
- conv_weight_grad: float32 [1792, 4], P(('ctx', 'head'))
- conv_bias_grad: float32 [1792], P(('ctx', 'head'))
- dt_bias_grad: float32 [24], P('head')
- a_log_grad: float32 [24], P('head')
- skip_grad: float32 [24], P('head')
The draws below stay inside these ranges and needn't reach their ends.
All inputs are finite; a program needn't handle non-finite values.
Results may differ from the reference program's by a relative error of at most 0.018.
The reference program's roundings to bfloat16 on the way count: a program that leaves them out, or rounds other values in their place, can miss the bound.
Values may be sent and summed in bfloat16 or wider, within the bound.
A program may use at most 192 MiB of HBM per device.

```python
import math
import jax
import jax.numpy as jnp
from jax import lax

D = 1024
FF = 2048
MH = 24
MP = 64
NS = 128
KW = 4
AH = 8
KVH = 2
HDIM = 64
SB = 256
TOK_DEV = 128
L = 4096
DSSM = 1536
CONVCH = 1792
NPROJ = 4120
NOUT = 2048
N_HEAD = 4


def shared_pattern(key):
    base = jax.random.fold_in(key, 9001)
    rate_dir = jnp.where(jax.random.bernoulli(jax.random.fold_in(base, 3), 0.5, (D,)), 1.0, -1.0).astype(jnp.float32)
    return rate_dir


def range_offsets(key):
    range_rows = TOK_DEV * N_HEAD
    ranges = L // range_rows
    base = jax.random.fold_in(key, 7001)
    order = jax.random.permutation(jax.random.fold_in(base, 1), ranges).astype(jnp.float32)
    jitter = jax.random.uniform(jax.random.fold_in(base, 2), (ranges,), jnp.float32)
    levels = -1.0 + 2.0 * (order + jitter) / ranges
    return jnp.repeat(levels, range_rows)


def draw_x_in(key, part):
    rate_dir = shared_pattern(key)
    offsets = range_offsets(key)[:, None] * rate_dir[None, :]
    values = jax.random.normal(jax.random.fold_in(key, 1), (L, D), jnp.float32) + offsets
    return jnp.clip(values, -6.0, 6.0).astype(jnp.bfloat16)


def draw_in_weight(key, part):
    values = jnp.clip(jax.random.normal(jax.random.fold_in(key, 2), (D, NPROJ), jnp.float32), -6.0, 6.0) / math.sqrt(D)
    rate_dir = shared_pattern(key)
    rate_start = 2 * MH * MP + 2 * NS
    rate_extra = 4.0 * rate_dir[:, None] * jnp.ones((1, MH), jnp.float32) / D
    values = jnp.concatenate([values[:, :rate_start], values[:, rate_start:rate_start + MH] + rate_extra, values[:, rate_start + MH:]], axis=1)
    return jnp.clip(values, -1.0, 1.0).astype(jnp.bfloat16)


def steps_of(rng, shape, cuts, smallest, largest):
    factor_of = 1.0
    for dim, shards_of in cuts:
        draws = jax.random.uniform(jax.random.fold_in(jax.random.fold_in(rng, 6), dim), (shards_of,), jnp.float32, smallest / len(cuts), largest / len(cuts))
        factor_of = factor_of * jnp.repeat(jnp.exp(draws), shape[dim] // shards_of).reshape((-1,) + (1,) * (len(shape) - 1 - dim))
    return factor_of


def noise(stream_key, shape, width, most, split=(), dtype=jnp.bfloat16):
    values = width * jax.random.normal(stream_key, shape, jnp.float32)
    if split:
        values = values * steps_of(stream_key, shape, split, -0.22, 0.18)
    return jnp.clip(values, -most, most).astype(dtype)


def setup_inputs(seed: int = 0) -> dict:
    seeds = jax.random.split(jax.random.key(seed), 15)
    return {
        "x_in": draw_x_in(jax.random.fold_in(seeds[14], 71), 0),
        "in_weight": draw_in_weight(jax.random.fold_in(seeds[14], 71), 0),
        "out_weight": noise(seeds[2], (NOUT, D), (NOUT // 2) ** -0.5, 0.1875, ((0, 32),)),
        "gu_weight": noise(seeds[3], (D, 2 * FF), D ** -0.5, 0.1875, ((0, 32),)),
        "down_weight": noise(seeds[4], (FF, D), FF ** -0.5, 0.125, ((0, 32),)),
        "norm_gain": jnp.clip(1.0 + 0.1 * jax.random.normal(seeds[5], (D,), jnp.float32), 0.5, 1.5).astype(jnp.bfloat16),
        "mixer_gain": jnp.clip(1.0 + 0.1 * jax.random.normal(seeds[6], (DSSM,), jnp.float32), 0.5, 1.5).astype(jnp.bfloat16),
        "ffn_gain": jnp.clip(1.0 + 0.1 * jax.random.normal(seeds[7], (D,), jnp.float32), 0.5, 1.5).astype(jnp.bfloat16),
        "conv_weight": noise(seeds[8], (CONVCH, KW), KW ** -0.5, 3.0, ((0, 32),)),
        "conv_bias": noise(seeds[9], (CONVCH,), 0.5, 3.0, ((0, 32),)),
        "dt_bias": jnp.clip(jax.random.uniform(seeds[10], (MH,), jnp.float32, -1.0, 1.0) * steps_of(seeds[10], (MH,), ((0, 4),), -0.4, 0.0), -1.0, 1.0),
        "a_log": jnp.clip(-14.0 + 12.0 * jax.random.uniform(seeds[11], (MH,), jnp.float32) ** steps_of(seeds[11], (MH,), ((0, 4),), -0.2, 0.2), -14.0, -2.0),
        "skip_gain": jnp.clip(2.0 * jax.random.uniform(seeds[12], (MH,), jnp.float32) ** steps_of(seeds[12], (MH,), ((0, 4),), -0.2, 0.2), 0.0, 2.0),
        "out_grad": noise(seeds[13], (L, D), 1.0, 6.0, ((0, 32),)),
    }


EPSILON = 1e-05
ROPE_BASE = 10000.0
PRECISE_MODE = lax.Precision.HIGHEST

def silu_grad(value):
    sigmoid = jax.nn.sigmoid(value)
    return sigmoid * (1.0 + value * (1.0 - sigmoid))

def rotate_pairs(values, positions, direction):
    half_dim = values.shape[-1] // 2
    inverse = ROPE_BASE ** (-jnp.arange(half_dim).astype(jnp.float32) / half_dim)
    angles = positions[:, None] * inverse[None, :]
    cosine = jnp.cos(angles)[:, None, :]
    sine = direction * jnp.sin(angles)[:, None, :]
    first_half = values[..., :half_dim]
    second_half = values[..., half_dim:]
    return jnp.concatenate([first_half * cosine - second_half * sine, second_half * cosine + first_half * sine], axis=-1)

def state_block(state, pieces, decay_rate, skip_gain):
    inputs_x, bmat, cmat, step_size = pieces
    length = inputs_x.shape[0]
    cumulative = jnp.cumsum(step_size * decay_rate[None, :], axis=0)
    lower = (jnp.arange(length)[:, None] >= jnp.arange(length)[None, :])[None, :, :]
    spread = cumulative.T[:, :, None] - cumulative.T[:, None, :]
    within = jnp.where(lower, jnp.exp(jnp.where(lower, spread, 0.0)), 0.0)
    scaled_x = inputs_x * step_size[:, :, None]
    products = jnp.dot(cmat, bmat.T, precision=PRECISE_MODE)
    intra = jnp.einsum('ts,hts,shp->thp', products, within, scaled_x, precision=PRECISE_MODE)
    inter = jnp.einsum('tn,hpn->thp', cmat, state, precision=PRECISE_MODE) * jnp.exp(cumulative)[:, :, None]
    remain = jnp.exp(cumulative[-1][None, :] - cumulative)
    new_state = jnp.exp(cumulative[-1])[:, None, None] * state + jnp.einsum('sh,shp,sn->hpn', remain, scaled_x, bmat, precision=PRECISE_MODE)
    return (new_state, intra + inter + skip_gain[None, :, None] * inputs_x)

def mixer_local(inputs_x, bmat, cmat, step_size, decay_rate, skip_gain, state):
    count = inputs_x.shape[0] // SB

    def advance(carry, pieces):
        return state_block(carry, pieces, decay_rate, skip_gain)

    def shaped(value):
        return value.reshape((count, SB) + value.shape[1:])
    final, outputs = lax.scan(advance, state, (shaped(inputs_x), shaped(bmat), shaped(cmat), shaped(step_size)))
    return (outputs.reshape(inputs_x.shape), final)

def reference(x_in, in_weight, out_weight, gu_weight, down_weight, norm_gain, mixer_gain, ffn_gain, conv_weight, conv_bias, dt_bias, a_log, skip_gain, out_grad):
    float_type = jnp.float32
    half_type = jnp.bfloat16
    total = x_in.shape[0]
    dssm_cols = MH * MP
    conv_cols = dssm_cols + 2 * NS
    query_start = 2 * dssm_cols + 2 * NS + MH
    key_start = query_start + AH * HDIM
    value_start = key_start + KVH * HDIM
    group_size = AH // KVH
    score_scale = 1.0 / math.sqrt(HDIM)
    block_rows = 512
    block_count = total // block_rows
    inputs = x_in.astype(float_type)
    gain_one = norm_gain.astype(float_type)
    gain_mix = mixer_gain.astype(float_type)
    gain_two = ffn_gain.astype(float_type)
    conv_w = conv_weight.astype(float_type)
    conv_b = conv_bias.astype(float_type)
    rms_in = lax.rsqrt(lax.optimization_barrier(jnp.mean(inputs * inputs, axis=1, keepdims=True)) + EPSILON)
    normed = (inputs * rms_in * gain_one[None, :]).astype(half_type)
    proj = jnp.dot(normed, in_weight, preferred_element_type=float_type).astype(half_type)
    z_part = proj[:, :dssm_cols].astype(float_type)
    padded = jnp.concatenate([jnp.zeros((KW - 1, conv_cols), float_type), proj[:, dssm_cols:dssm_cols + conv_cols].astype(float_type)], axis=0)
    conv_pre = jnp.broadcast_to(conv_b[None, :], (total, conv_cols))
    for offset in range(KW):
        conv_pre = conv_pre + padded[offset:offset + total] * conv_w[:, offset][None, :]
    conv_out = jax.nn.silu(conv_pre).astype(half_type)
    mix_x = conv_out[:, :dssm_cols].astype(float_type).reshape(total, MH, MP)
    bmat = conv_out[:, dssm_cols:dssm_cols + NS].astype(float_type)
    cmat = conv_out[:, dssm_cols + NS:].astype(float_type)
    dt_pre = proj[:, dssm_cols + conv_cols:query_start].astype(float_type) + dt_bias[None, :]
    step_size = jax.nn.softplus(dt_pre)
    decay_rate = -jnp.exp(a_log)

    def mixer_map(mix_in, b_in, c_in, step_in, decay_in, skip_in):
        return mixer_local(mix_in, b_in, c_in, step_in, decay_in, skip_in, jnp.zeros((MH, MP, NS), float_type))[0]
    ssm_full, ssm_pull = jax.vjp(mixer_map, mix_x, bmat, cmat, step_size, decay_rate, skip_gain)
    ssm_out = ssm_full.reshape(total, dssm_cols).astype(half_type)
    positions = jnp.arange(total).astype(float_type)
    q_rot = rotate_pairs(proj[:, query_start:key_start].astype(float_type).reshape(total, AH, HDIM), positions, 1.0).astype(half_type)
    k_rot = rotate_pairs(proj[:, key_start:value_start].astype(float_type).reshape(total, KVH, HDIM), positions, 1.0).astype(half_type)
    keys_all = jnp.repeat(k_rot, group_size, axis=1).astype(float_type)
    values_all = jnp.repeat(proj[:, value_start:].reshape(total, KVH, HDIM), group_size, axis=1).astype(float_type)
    queries_all = q_rot.astype(float_type)

    def block_scores(query_blk, key_blk, query_first, key_first):
        raw = jnp.einsum('thd,uhd->thu', query_blk, key_blk) * score_scale
        valid = (key_first + jnp.arange(block_rows))[None, None, :] <= (query_first + jnp.arange(block_rows))[:, None, None]
        return jnp.where(valid, raw, -jnp.inf)

    def attend(number):
        query_first = number * block_rows
        query_blk = lax.dynamic_slice_in_dim(queries_all, query_first, block_rows, 0)

        def stat_step(other, carry):
            row_peak, row_mass = carry
            scores = block_scores(query_blk, lax.dynamic_slice_in_dim(keys_all, other * block_rows, block_rows, 0), query_first, other * block_rows)
            new_peak = jnp.maximum(row_peak, lax.optimization_barrier(jnp.max(scores, axis=2)))
            row_mass = row_mass * jnp.exp(row_peak - new_peak) + lax.optimization_barrier(jnp.sum(jnp.exp(scores - new_peak[:, :, None]), axis=2))
            return (new_peak, row_mass)
        row_peak, row_mass = lax.fori_loop(0, number + 1, stat_step, (jnp.full((block_rows, AH), -jnp.inf, float_type), jnp.zeros((block_rows, AH), float_type)))
        log_total = row_peak + jnp.log(row_mass)

        def out_step(other, accum):
            scores = block_scores(query_blk, lax.dynamic_slice_in_dim(keys_all, other * block_rows, block_rows, 0), query_first, other * block_rows)
            probs = lax.optimization_barrier(jnp.exp(scores - log_total[:, :, None]).astype(half_type)).astype(float_type)
            return accum + jnp.einsum('thu,uhd->thd', probs, lax.dynamic_slice_in_dim(values_all, other * block_rows, block_rows, 0))
        attn_blk = lax.fori_loop(0, number + 1, out_step, jnp.zeros((block_rows, AH, HDIM), float_type))
        return (attn_blk.astype(half_type), log_total)
    attn_blocks, log_blocks = lax.map(attend, jnp.arange(block_count))
    attn = attn_blocks.reshape(total, AH * HDIM)
    log_all = log_blocks.reshape(total, AH)
    gated = ssm_out.astype(float_type) * jax.nn.silu(z_part)
    rms_mix = lax.rsqrt(lax.optimization_barrier(jnp.mean(gated * gated, axis=1, keepdims=True)) + EPSILON)
    mixed_norm = (gated * rms_mix * gain_mix[None, :]).astype(half_type)
    joined = jnp.concatenate([mixed_norm, attn], axis=1)
    residual = inputs + jnp.dot(joined, out_weight, preferred_element_type=float_type)
    rms_ffn = lax.rsqrt(lax.optimization_barrier(jnp.mean(residual * residual, axis=1, keepdims=True)) + EPSILON)
    normed_ffn = (residual * rms_ffn * gain_two[None, :]).astype(half_type)
    gate_up = jnp.dot(normed_ffn, gu_weight, preferred_element_type=float_type)
    gate_part = gate_up[:, :FF]
    up_part = gate_up[:, FF:]
    activ = (jax.nn.silu(gate_part) * up_part).astype(half_type)
    y_out = (residual + jnp.dot(activ, down_weight, preferred_element_type=float_type)).astype(half_type)
    d_activ = jnp.dot(out_grad, down_weight.T, preferred_element_type=float_type)
    down_grad = jnp.dot(activ.T, out_grad, preferred_element_type=float_type)
    d_gate_up = jnp.concatenate([d_activ * up_part * silu_grad(gate_part), d_activ * jax.nn.silu(gate_part)], axis=1).astype(half_type)
    d_normed_ffn = jnp.dot(d_gate_up, gu_weight.T, preferred_element_type=float_type)
    gu_grad = jnp.dot(normed_ffn.T, d_gate_up, preferred_element_type=float_type)
    ffn_gain_grad = lax.optimization_barrier(jnp.sum(d_normed_ffn * residual * rms_ffn, axis=0))
    scaled_ffn = gain_two[None, :] * d_normed_ffn
    d_residual = out_grad.astype(float_type) + rms_ffn * scaled_ffn - residual * rms_ffn ** 3 * lax.optimization_barrier(jnp.mean(scaled_ffn * residual, axis=1, keepdims=True))
    d_res_half = d_residual.astype(half_type)
    d_joined = jnp.dot(d_res_half, out_weight.T, preferred_element_type=float_type)
    out_weight_grad = jnp.dot(joined.T, d_res_half, preferred_element_type=float_type)
    d_mixed = d_joined[:, :dssm_cols]
    d_attn = d_joined[:, dssm_cols:].astype(half_type)
    mixer_gain_grad = lax.optimization_barrier(jnp.sum(d_mixed * gated * rms_mix, axis=0))
    scaled_mix = gain_mix[None, :] * d_mixed
    d_gated = rms_mix * scaled_mix - gated * rms_mix ** 3 * lax.optimization_barrier(jnp.mean(scaled_mix * gated, axis=1, keepdims=True))
    d_ssm = (d_gated * jax.nn.silu(z_part)).astype(half_type)
    d_z = d_gated * ssm_out.astype(float_type) * silu_grad(z_part)
    d_attn_all = d_attn.astype(float_type).reshape(total, AH, HDIM)
    row_delta = lax.optimization_barrier(jnp.sum(d_attn_all * attn.astype(float_type).reshape(total, AH, HDIM), axis=2))

    def back_block(carry, number):
        key_grads, value_grads = carry
        query_first = number * block_rows
        query_blk = lax.dynamic_slice_in_dim(queries_all, query_first, block_rows, 0)
        grad_blk = lax.dynamic_slice_in_dim(d_attn_all, query_first, block_rows, 0)
        log_blk = lax.dynamic_slice_in_dim(log_all, query_first, block_rows, 0)
        delta_blk = lax.dynamic_slice_in_dim(row_delta, query_first, block_rows, 0)

        def inner(other, state):
            query_grad, key_acc, value_acc = state
            key_first = other * block_rows
            key_blk = lax.dynamic_slice_in_dim(keys_all, key_first, block_rows, 0)
            value_blk = lax.dynamic_slice_in_dim(values_all, key_first, block_rows, 0)
            probs = jnp.exp(block_scores(query_blk, key_blk, query_first, key_first) - log_blk[:, :, None])
            probs_half = lax.optimization_barrier(probs.astype(half_type)).astype(float_type)
            d_probs = jnp.einsum('thd,uhd->thu', grad_blk, value_blk)
            d_scores = lax.optimization_barrier((probs * (d_probs - delta_blk[:, :, None])).astype(half_type)).astype(float_type)
            query_grad = query_grad + jnp.einsum('thu,uhd->thd', d_scores, key_blk) * score_scale
            key_part = jnp.einsum('thu,thd->uhd', d_scores, query_blk) * score_scale
            value_part = jnp.einsum('thu,thd->uhd', probs_half, grad_blk)
            key_acc = lax.dynamic_update_slice_in_dim(key_acc, lax.dynamic_slice_in_dim(key_acc, key_first, block_rows, 0) + key_part, key_first, 0)
            value_acc = lax.dynamic_update_slice_in_dim(value_acc, lax.dynamic_slice_in_dim(value_acc, key_first, block_rows, 0) + value_part, key_first, 0)
            return (query_grad, key_acc, value_acc)
        query_grad, key_grads, value_grads = lax.fori_loop(0, number + 1, inner, (jnp.zeros((block_rows, AH, HDIM), float_type), key_grads, value_grads))
        return ((key_grads, value_grads), query_grad)
    zero_keys = jnp.zeros((total, AH, HDIM), float_type)
    (key_grads, value_grads), query_grads = lax.scan(back_block, (zero_keys, zero_keys), jnp.arange(block_count))
    d_query = rotate_pairs(query_grads.reshape(total, AH, HDIM), positions, -1.0).reshape(total, AH * HDIM)
    d_key = rotate_pairs(lax.optimization_barrier(jnp.sum(key_grads.reshape(total, KVH, group_size, HDIM), axis=2)), positions, -1.0).reshape(total, KVH * HDIM)
    d_value = lax.optimization_barrier(jnp.sum(value_grads.reshape(total, KVH, group_size, HDIM), axis=2)).reshape(total, KVH * HDIM)
    grad_x, grad_b, grad_c, grad_step, grad_decay, skip_grad = ssm_pull(d_ssm.astype(float_type).reshape(total, MH, MP))
    d_dt_pre = grad_step * jax.nn.sigmoid(dt_pre)
    dt_bias_grad = lax.optimization_barrier(jnp.sum(d_dt_pre, axis=0))
    a_log_grad = grad_decay * decay_rate
    d_conv_pre = jnp.concatenate([grad_x.reshape(total, dssm_cols), grad_b, grad_c], axis=1) * silu_grad(conv_pre)
    conv_bias_grad = lax.optimization_barrier(jnp.sum(d_conv_pre, axis=0))
    conv_weight_grad = jnp.stack([lax.optimization_barrier(jnp.sum(d_conv_pre * padded[offset:offset + total], axis=0)) for offset in range(KW)], axis=1)
    d_padded = jnp.zeros((total + KW - 1, conv_cols), float_type)
    for offset in range(KW):
        d_padded = d_padded + jnp.pad(d_conv_pre * conv_w[:, offset][None, :], ((offset, KW - 1 - offset), (0, 0)))
    d_xbc = d_padded[KW - 1:]
    d_proj = jnp.concatenate([d_z, d_xbc, d_dt_pre, d_query, d_key, d_value], axis=1).astype(half_type)
    d_normed = jnp.dot(d_proj, in_weight.T, preferred_element_type=float_type)
    in_grad = jnp.dot(normed.T, d_proj, preferred_element_type=float_type)
    norm_gain_grad = lax.optimization_barrier(jnp.sum(d_normed * inputs * rms_in, axis=0))
    scaled_in = gain_one[None, :] * d_normed
    x_grad = d_residual + rms_in * scaled_in - inputs * rms_in ** 3 * lax.optimization_barrier(jnp.mean(scaled_in * inputs, axis=1, keepdims=True))
    return (y_out, x_grad, in_grad, out_weight_grad, gu_grad, down_grad, norm_gain_grad, mixer_gain_grad, ffn_gain_grad, conv_weight_grad, conv_bias_grad, dt_bias_grad, a_log_grad, skip_grad)
```

```python
import functools
import math

import jax
import jax.numpy as jnp
import numpy as np
from jax import lax
from jax.experimental import pallas as pl
from jax.experimental.pallas import tpu as pltpu
from jax.sharding import PartitionSpec as P

FF = 2048
MH = 24
MP = 64
NS = 128
KW = 4
AH = 8
KVH = 2
HDIM = 64
CHUNK = 128


EPSILON = 1e-05
ROPE_BASE = 10000.0
PRECISE_MODE = lax.Precision.HIGHEST


def passed_along(block, axis, distance):
    devices = range(lax.axis_size(axis))
    route = [(i - distance, i) for i in devices if i - distance in devices]
    return lax.ppermute(block, axis, route)


def silu_grad(value):
    sigmoid = jax.nn.sigmoid(value)
    return sigmoid * (1.0 + value * (1.0 - sigmoid))


def rotate_pairs(values, positions, direction):
    half_dim = values.shape[-1] // 2
    inverse = ROPE_BASE ** (-jnp.arange(half_dim).astype(jnp.float32) / half_dim)
    angles = positions[:, None] * inverse[None, :]
    cosine = jnp.cos(angles)[:, None, :]
    sine = direction * jnp.sin(angles)[:, None, :]
    first_half = values[..., :half_dim]
    second_half = values[..., half_dim:]
    return jnp.concatenate(
        [first_half * cosine - second_half * sine, second_half * cosine + first_half * sine],
        axis=-1,
    )


def dot_back(first_op, second_op):
    return lax.dot_general(
        first_op, second_op, (((1,), (1,)), ((), ())), preferred_element_type=jnp.float32
    )


def dot_rows(first_op, second_op):
    return lax.dot_general(
        first_op, second_op, (((0,), (0,)), ((), ())), preferred_element_type=jnp.float32
    )


def spread_to_all(block, axis):
    size = lax.axis_size(axis)
    copies = jnp.broadcast_to(block[None], (size,) + block.shape)
    return lax.all_to_all(copies, axis, split_axis=0, concat_axis=0, tiled=True)


def summed_parts(stacked, axis):
    got = lax.all_to_all(stacked, axis, split_axis=0, concat_axis=0, tiled=True)
    return jnp.sum(got.astype(jnp.float32), axis=0)


def ein(spec, first_op, second_op):
    return jnp.einsum(
        spec,
        first_op.astype(jnp.bfloat16),
        second_op.astype(jnp.bfloat16),
        preferred_element_type=jnp.float32,
    )


def ein_fine(spec, first_op, second_op):
    coarse = lax.reduce_precision(second_op, 8, 7)
    return ein(spec, first_op, coarse) + ein(spec, first_op, second_op - coarse)


MESH = pl.DeviceIdType.MESH
MIB = 1024 * 1024


def row_matchings(devices, heads):
    ranges = devices // heads
    chunks = devices * 4
    mixed = chunks * 3 // 4
    goal = []
    for k in range(chunks):
        if k < mixed:
            per_group = mixed // heads
            group, inner = divmod(k, per_group)
        else:
            group, inner = divmod(k - mixed, ranges)
            inner += mixed // heads
        piece, slot = divmod(inner, 4)
        goal.append((piece * heads + group, slot))
    left = [list(range(4 * b, 4 * b + 4)) for b in range(devices)]
    rounds = []
    for _ in range(4):
        taken = {}

        def place(b, seen):
            for k in left[b]:
                dest = goal[k][0]
                if dest in seen:
                    continue
                seen.add(dest)
                if dest not in taken or place(taken[dest] // 4, seen):
                    taken[dest] = k
                    return True
            return False

        for b in range(devices):
            place(b, set())
        sends = [0] * devices
        lands = [0] * devices
        route = []
        for dest in range(devices):
            k = taken[dest]
            b = k // 4
            left[b].remove(k)
            sends[b] = k % 4
            lands[dest] = goal[k][1]
            route.append((b, dest))
        rounds.append((route, sends, lands))
    return rounds


OUTER = 4


def ctx_grid():
    inner = lax.axis_size("ctx") // OUTER
    me = lax.axis_index("ctx")
    return inner, me, me // inner, lax.rem(me, inner)


def ctx_copy(source, target, send_sem, recv_sem, place):
    return pltpu.make_async_remote_copy(
        src_ref=source,
        dst_ref=target,
        send_sem=send_sem,
        recv_sem=recv_sem,
        device_id={"ctx": place},
        device_id_type=MESH,
    )


def greet_ctx(others=()):
    inner, _, far, near = ctx_grid()
    barrier = pltpu.get_barrier_semaphore()
    for o in range(1, OUTER):
        pl.semaphore_signal(
            barrier,
            inc=1,
            device_id={"ctx": lax.rem(far + o, OUTER) * inner + near},
            device_id_type=MESH,
        )
    for i in range(1, inner):
        pl.semaphore_signal(
            barrier,
            inc=1,
            device_id={"ctx": far * inner + lax.rem(near + i, inner)},
            device_id_type=MESH,
        )
    for peer in others:
        pl.semaphore_signal(barrier, inc=1, device_id={"head": peer}, device_id_type=MESH)
    pl.semaphore_wait(barrier, OUTER - 1 + inner - 1 + len(others))


class LineGather:
    def __init__(self, own_ref, all_ref, sems, number):
        self.own = own_ref
        self.all = all_ref
        (self.up_send, self.up_recv, self.down_send, self.down_recv) = (
            sem.at[number] for sem in sems[:4]
        )
        self.near_send, self.near_recv = (sem.at[number] for sem in sems[4:6])
        self.inner, self.me, self.far, self.near = ctx_grid()

    @staticmethod
    def scratch(count, inner):
        line = pltpu.SemaphoreType.DMA((count, OUTER - 1))
        near = pltpu.SemaphoreType.DMA((count, 2 * OUTER - 1, inner))
        return [line, line, line, line, near, near]

    def source(self, far, own):
        if own:
            return self.own
        return self.all.at[far * self.inner + self.near]

    def hop(self, t, way):
        shard = self.far - way * t
        sends, recvs = (
            (self.up_send, self.up_recv) if way == 1 else (self.down_send, self.down_recv)
        )
        return ctx_copy(
            self.source(shard, t == 0),
            self.all.at[shard * self.inner + self.near],
            sends.at[t],
            recvs.at[t],
            (self.far + way) * self.inner + self.near,
        )

    def arrives(self, t, way):
        return self.far >= t + 1 if way == 1 else self.far + 1 + t <= OUTER - 1

    def leaves(self, t, way):
        if way == 1:
            return jnp.logical_and(self.far < OUTER - 1, self.far >= t)
        return jnp.logical_and(self.far > 0, self.far + t <= OUTER - 1)

    def near_copies(self, slot, far):
        return [
            ctx_copy(
                self.source(far, slot == 0),
                self.all.at[far * self.inner + self.near],
                self.near_send.at[slot, i],
                self.near_recv.at[slot, i],
                self.far * self.inner + lax.rem(self.near + i, self.inner),
            )
            for i in range(1, self.inner)
        ]

    def begin(self):
        for way in (1, -1):

            @pl.when(self.leaves(0, way))
            def _():
                self.hop(0, way).start()

        for copy in self.near_copies(0, self.far):
            copy.start()

    def step(self, t):
        for way in (1, -1):

            @pl.when(self.arrives(t, way))
            def _():
                self.hop(t, way).wait_recv()
                if t + 1 < OUTER - 1:

                    @pl.when(self.leaves(t + 1, way))
                    def _():
                        self.hop(t + 1, way).start()

                for copy in self.near_copies(self.slot(t, way), self.far - way * (t + 1)):
                    copy.start()

    def slot(self, t, way):
        return 1 + t if way == 1 else OUTER + t

    def finish(self):
        for copy in self.near_copies(0, self.far):
            copy.wait()
        for way in (1, -1):
            for t in range(OUTER - 1):

                @pl.when(self.leaves(t, way))
                def _():
                    self.hop(t, way).wait_send()

                @pl.when(self.arrives(t, way))
                def _():
                    shard = self.far - way * (t + 1)
                    for copy in self.near_copies(self.slot(t, way), shard):
                        copy.wait()


def greet_line(others=()):
    inner, _, far, near = ctx_grid()
    barrier = pltpu.get_barrier_semaphore()
    places = [lax.rem(far + o, OUTER) * inner + near for o in (1, OUTER - 1)]
    places += [far * inner + lax.rem(near + i, inner) for i in range(1, inner)]
    for place in places:
        pl.semaphore_signal(barrier, inc=1, device_id={"ctx": place}, device_id_type=MESH)
    for peer in others:
        pl.semaphore_signal(barrier, inc=1, device_id={"head": peer}, device_id_type=MESH)
    pl.semaphore_wait(barrier, len(places) + len(others))


def gather_kernel(count, *refs):
    own_refs, all_refs = refs[:count], refs[count : 2 * count]
    local_sem = refs[2 * count]
    greet_line()
    _, me, _, _ = ctx_grid()
    works = [
        LineGather(own_refs[a], all_refs[a], refs[2 * count + 1 :], a) for a in range(count)
    ]
    local = [
        pltpu.make_async_copy(own_refs[a], all_refs[a].at[me], local_sem.at[a])
        for a in range(count)
    ]
    for work in works:
        work.begin()
    for copy in local:
        copy.start()
    for t in range(OUTER - 1):
        for work in works:
            work.step(t)
    for work in works:
        work.finish()
    for copy in local:
        copy.wait()


def gather_ctx(collective_id, *arrays):
    ranges = lax.axis_size("ctx")
    count = len(arrays)
    anywhere = pl.BlockSpec(memory_space=pl.ANY)
    size = sum(a.size * a.dtype.itemsize for a in arrays)
    return pl.pallas_call(
        functools.partial(gather_kernel, count),
        out_shape=tuple(jax.ShapeDtypeStruct((ranges,) + a.shape, a.dtype) for a in arrays),
        in_specs=[anywhere] * count,
        out_specs=[anywhere] * count,
        scratch_shapes=[pltpu.SemaphoreType.DMA((count,))]
        + LineGather.scratch(count, ranges // OUTER),
        compiler_params=pltpu.CompilerParams(collective_id=collective_id, has_side_effects=True),
        cost_estimate=pl.CostEstimate(
            flops=0, bytes_accessed=2 * ranges * size, transcendentals=0
        ),
    )(*arrays)


def front_kernel(heads, *refs):
    (in_ref, gu_ref, small_ref, out_ref, x_ref, grad_ref) = refs[:6]
    (in_all, gu_own, small_all, out_all, x_all, grad_all) = refs[6:12]
    local_sem, head_send, head_recv = refs[12:15]
    sems = refs[15:]
    me = lax.axis_index("head")
    peers = [lax.rem(me + p, heads) for p in range(1, heads)]
    _, place, _, _ = ctx_grid()
    greet_line(peers)

    def to_peer(n, p, source, target):
        return pltpu.make_async_remote_copy(
            src_ref=source,
            dst_ref=target,
            send_sem=head_send.at[n, p],
            recv_sem=head_recv.at[n, p],
            device_id={"head": peers[p - 1]},
            device_id_type=MESH,
        )

    out_work = LineGather(out_ref, out_all, sems, 0)
    out_work.begin()
    local = []

    def exchange(n, source, target, split=False):
        copy = pltpu.make_async_copy(source.at[me] if split else source, target, local_sem.at[n])
        copy.start()
        sent = [
            to_peer(n, p, source.at[peers[p - 1]] if split else source, target)
            for p in range(1, heads)
        ]
        for one in sent:
            one.start()
        return [copy] + sent

    in_sent = exchange(0, in_ref, in_all.at[place, me], True)
    small_sent = exchange(2, small_ref, small_all.at[place, me])
    copy = pltpu.make_async_copy(out_ref, out_all.at[place], local_sem.at[5])
    copy.start()
    local.append(copy)
    works = [out_work]
    for n, (sent, target) in enumerate(((in_sent, in_all), (small_sent, small_all))):
        for copy in sent:
            copy.wait()
        work = LineGather(target.at[place], target, sems, 1 + n)
        work.begin()
        works.append(work)
    local += exchange(3, x_ref, x_all.at[me])
    local += exchange(1, gu_ref, gu_own.at[me], True)
    local += exchange(4, grad_ref, grad_all.at[me])
    for t in range(OUTER - 1):
        for work in works:
            work.step(t)
    for work in works:
        work.finish()
    for copy in local:
        copy.wait()


def front(heads, in_cols, gu_cols, small, out_rows, x_in, out_grad):
    ranges = lax.axis_size("ctx")
    anywhere = pl.BlockSpec(memory_space=pl.ANY)
    half = jnp.bfloat16
    shapes = (
        (ranges,) + in_cols.shape,
        gu_cols.shape,
        (ranges, heads) + small.shape,
        (ranges,) + out_rows.shape,
        (heads,) + x_in.shape,
        (heads,) + out_grad.shape,
    )
    size = sum(math.prod(shape) for shape in shapes)
    return pl.pallas_call(
        functools.partial(front_kernel, heads),
        out_shape=tuple(jax.ShapeDtypeStruct(shape, half) for shape in shapes),
        in_specs=[anywhere] * 6,
        out_specs=[anywhere] * 6,
        scratch_shapes=[
            pltpu.SemaphoreType.DMA((7,)),
            pltpu.SemaphoreType.DMA((5, heads)),
            pltpu.SemaphoreType.DMA((5, heads)),
        ]
        + LineGather.scratch(3, ranges // OUTER),
        compiler_params=pltpu.CompilerParams(collective_id=1, has_side_effects=True),
        cost_estimate=pl.CostEstimate(flops=0, bytes_accessed=4 * size, transcendentals=0),
    )(in_cols, gu_cols, small, out_rows, x_in, out_grad)


class Scatter:
    def __init__(self, part_ref, rows, scratch, first=0, size=None):
        self.part = part_ref
        self.rows = rows
        self.first = first
        self.size = rows if size is None else size
        (self.got_near, self.sums, self.got_far, self.own) = scratch[:4]
        (self.near_send, self.near_recv, self.far_send, self.far_recv) = scratch[4:]
        self.inner, self.me, self.far, self.near = ctx_grid()
        self.near_copies = {}
        self.far_copies = {}

    @staticmethod
    def scratch(rows, cols, inner, dtype=jnp.bfloat16):
        return [
            pltpu.VMEM((inner, OUTER, rows, cols), dtype),
            pltpu.VMEM((OUTER, rows, cols), dtype),
            pltpu.VMEM((OUTER, rows, cols), dtype),
            pltpu.VMEM((rows, cols), jnp.float32),
            pltpu.SemaphoreType.DMA((inner, OUTER)),
            pltpu.SemaphoreType.DMA((inner, OUTER)),
            pltpu.SemaphoreType.DMA((OUTER,)),
            pltpu.SemaphoreType.DMA((OUTER,)),
        ]

    def block(self, far, near):
        at = (far * self.inner + near) * self.rows + self.first
        return pl.ds(pl.multiple_of(at, self.size), self.size)

    def start(self, o):
        far = lax.rem(self.far + o, OUTER)
        for i in range(1, self.inner):
            near = lax.rem(self.near + i, self.inner)
            copy = ctx_copy(
                self.part.at[self.block(far, near)],
                self.got_near.at[i, o],
                self.near_send.at[i, o],
                self.near_recv.at[i, o],
                self.far * self.inner + near,
            )
            copy.start()
            self.near_copies[i, o] = copy

    def pass_on(self, o):
        far = lax.rem(self.far + o, OUTER)
        for i in range(1, self.inner):
            self.near_copies[i, o].wait_recv()
        total = self.part[self.block(far, self.near), :].astype(jnp.float32)
        for i in range(1, self.inner):
            total = total + self.got_near[i, o].astype(jnp.float32)
        if o == 0:
            self.own[...] = total
            return
        self.sums[o] = total.astype(self.sums.dtype)
        copy = ctx_copy(
            self.sums.at[o],
            self.got_far.at[o],
            self.far_send.at[o],
            self.far_recv.at[o],
            far * self.inner + self.near,
        )
        copy.start()
        self.far_copies[o] = copy

    def finish(self, out_ref):
        total = self.own[...]
        for o in range(1, OUTER):
            self.far_copies[o].wait()
            total = total + self.got_far[o].astype(jnp.float32)
        out_ref[...] = total.reshape(out_ref.shape).astype(out_ref.dtype)
        for copy in self.near_copies.values():
            copy.wait_send()


def scatter_all(works, begun=0):
    steps = [(work, o) for o in list(range(1, OUTER)) + [0] for work in works]
    for work, o in steps[begun:2]:
        work.start(o)
    for n, (work, o) in enumerate(steps):
        work.pass_on(o)
        if n + 2 < len(steps):
            after, later = steps[n + 2]
            after.start(later)


def tail_kernel(heads, *refs):
    in_ref, small_ref, normed_ref, gu_ref, in_got, small_got, normed_got, gu_got = refs[:8]
    in_sum, small_sum, local_sem, head_send, head_recv = refs[8:13]
    me = lax.axis_index("head")
    peers = [lax.rem(me + p, heads) for p in range(1, heads)]
    greet_ctx(peers)
    running = []

    def exchange(n, source, target):
        copy = pltpu.make_async_copy(source.at[me], target.at[me], local_sem.at[n])
        copy.start()
        running.append(copy)
        for p in range(1, heads):
            one = pltpu.make_async_remote_copy(
                src_ref=source.at[peers[p - 1]],
                dst_ref=target.at[me],
                send_sem=head_send.at[n, p],
                recv_sem=head_recv.at[n, p],
                device_id={"head": peers[p - 1]},
                device_id_type=MESH,
            )
            one.start()
            running.append(one)

    exchange(0, normed_ref, normed_got)
    exchange(1, gu_ref, gu_got)
    rows = in_ref.shape[0] // lax.axis_size("ctx")
    works = [
        Scatter(in_ref, rows, refs[21 + 8 * n : 29 + 8 * n], n * rows // 2, rows // 2)
        for n in range(2)
    ]
    small_work = Scatter(small_ref, heads * 8, refs[13:21])
    scatter_all([small_work] + works)
    small_work.finish(small_sum)
    exchange(3, small_sum, small_got)
    for n, work in enumerate(works):
        work.finish(in_sum.at[pl.ds(n * heads // 2, heads // 2)])
    exchange(2, in_sum, in_got)
    for copy in running:
        copy.wait()


def tail(heads, in_grad, small_grads, normed_parts, gu_parts):
    ranges = lax.axis_size("ctx")
    half = jnp.bfloat16
    rows, cols = in_grad.shape[0] // ranges, in_grad.shape[1]
    in_shape = (heads, rows // heads, cols)
    vmem = pl.BlockSpec(memory_space=pltpu.VMEM)
    anywhere = pl.BlockSpec(memory_space=pl.ANY)
    return pl.pallas_call(
        functools.partial(tail_kernel, heads),
        out_shape=(
            jax.ShapeDtypeStruct(in_shape, half),
            jax.ShapeDtypeStruct((heads, 8, small_grads.shape[1]), jnp.float32),
            jax.ShapeDtypeStruct(normed_parts.shape, half),
            jax.ShapeDtypeStruct(gu_parts.shape, half),
        ),
        in_specs=[vmem, vmem, anywhere, anywhere],
        out_specs=[anywhere] * 4,
        scratch_shapes=[
            pltpu.VMEM(in_shape, half),
            pltpu.VMEM((heads, 8, small_grads.shape[1]), jnp.float32),
            pltpu.SemaphoreType.DMA((4,)),
            pltpu.SemaphoreType.DMA((4, heads)),
            pltpu.SemaphoreType.DMA((4, heads)),
        ]
        + Scatter.scratch(heads * 8, small_grads.shape[1], ranges // OUTER, jnp.float32)
        + Scatter.scratch(rows // 2, cols, ranges // OUTER) * 2,
        compiler_params=pltpu.CompilerParams(
            collective_id=2, has_side_effects=True, vmem_limit_bytes=40 * MIB
        ),
        cost_estimate=pl.CostEstimate(
            flops=2 * in_grad.size, bytes_accessed=6 * in_grad.size, transcendentals=0
        ),
    )(in_grad, small_grads, normed_parts, gu_parts)


def scatter_kernel(rows, part_ref, out_ref, *scratch):
    greet_ctx()
    work = Scatter(part_ref, rows, scratch)
    scatter_all([work])
    work.finish(out_ref)


def scatter_ctx(collective_id, part, dtype):
    ranges = lax.axis_size("ctx")
    rows, cols = part.shape[0] // ranges, part.shape[1]
    vmem = pl.BlockSpec(memory_space=pltpu.VMEM)
    return pl.pallas_call(
        functools.partial(scatter_kernel, rows),
        out_shape=jax.ShapeDtypeStruct((rows, cols), dtype),
        in_specs=[vmem],
        out_specs=vmem,
        scratch_shapes=Scatter.scratch(rows, cols, ranges // OUTER),
        compiler_params=pltpu.CompilerParams(
            collective_id=collective_id, has_side_effects=True, vmem_limit_bytes=40 * MIB
        ),
        cost_estimate=pl.CostEstimate(
            flops=2 * part.size, bytes_accessed=4 * part.size, transcendentals=0
        ),
    )(part)


def middle_kernel(
    heads,
    gated_ref,
    attn_ref,
    out_ref,
    gu_ref,
    down_ref,
    x_ref,
    grad_ref,
    gain_mix_ref,
    gain_two_ref,
    y_ref,
    d_res_ref,
    d_gated_ref,
    d_attn_ref,
    down_sum_ref,
    gu_sum_ref,
    out_sum_ref,
    mix_gain_grad_ref,
    ffn_gain_grad_ref,
    squares,
    pulls,
    mixed,
    part_a,
    got_a,
    normed_two,
    d_activ,
    activ,
    d_gate_up,
    part_b,
    got_b,
    part_c,
    got_c,
    d_res_all,
    d_mixed,
    down_grad_ref,
    gu_grad_ref,
    out_grad_ref,
    gu_all,
    down_all,
    send_sem,
    recv_sem,
    *scatter_scratch,
):
    ranges = lax.axis_size("ctx")
    down_work, gu_work, out_work = (
        Scatter(part, part.shape[0] // ranges, scatter_scratch[8 * n : 8 * n + 8])
        for n, part in enumerate((down_grad_ref, gu_grad_ref, out_grad_ref))
    )
    f32 = jnp.float32
    half = jnp.bfloat16
    me = lax.axis_index("head")
    rows, mine = gated_ref.shape
    tokens, width = x_ref.shape
    units = down_ref.shape[0] * ranges
    dssm = mine * heads
    tile = 256
    peers = [lax.rem(me + p, heads) for p in range(1, heads)]

    greet_ctx(peers)
    _, place, _, _ = ctx_grid()
    gathers = [
        LineGather(own, target, scatter_scratch[24:], n)
        for n, (own, target) in enumerate(((gu_ref, gu_all), (down_ref, down_all)))
    ]
    for gather in gathers:
        gather.begin()
    gu_all[place] = gu_ref[...]
    down_all[place] = down_ref[...]

    def gather_step(t):
        for gather in gathers:
            gather.step(t)

    def row_tile(whole, i):
        per = tile // whole.shape[1]
        return whole[pl.ds(i * per, per)].reshape(tile, whole.shape[2])

    wm_ref = out_ref.at[pl.ds(0, mine)]
    wa_ref = out_ref.at[pl.ds(mine, out_ref.shape[0] - mine)]

    def block(number):
        return pl.ds(pl.multiple_of(number * tokens, tokens), tokens)

    def tiles(count, body):
        def step(i, carry):
            body(pl.ds(pl.multiple_of(i * tile, tile), tile))
            return carry

        lax.fori_loop(0, count // tile, step, 0)

    def copies(slot, source, target):
        made = []
        for p in range(1, heads):
            made.append(
                pltpu.make_async_remote_copy(
                    src_ref=source(p),
                    dst_ref=target(p),
                    send_sem=send_sem.at[slot, p],
                    recv_sem=recv_sem.at[slot, p],
                    device_id={"head": peers[p - 1]},
                    device_id_type=MESH,
                )
            )
        for copy in made:
            copy.start()
        return made

    def settle(made):
        for copy in made:
            copy.wait()

    def row_totals(value):
        return lax.dot_general(
            jnp.ones((8, value.shape[1]), f32),
            value,
            (((1,), (1,)), ((), ())),
            preferred_element_type=f32,
            precision=PRECISE_MODE,
        )

    def as_column(buffer):
        total = buffer[0]
        for p in range(1, heads):
            total = total + buffer[p]
        spread = lax.dot_general(
            total,
            jnp.full((8, 128), 0.125, f32),
            (((0,), (0,)), ((), ())),
            preferred_element_type=f32,
            precision=PRECISE_MODE,
        )
        return spread[:, :1]

    gated = gated_ref[...]
    squares[0] = row_totals(gated * gated)
    first = copies(0, lambda p: squares.at[0], lambda p: squares.at[p])

    settle(first)
    rms_mix = lax.rsqrt(as_column(squares) / dssm + EPSILON)
    gain_mix = gain_mix_ref[...]
    mixed[...] = (gated * rms_mix * gain_mix).astype(half)

    def out_tile(at):
        part_a[:, at] = (
            jnp.dot(mixed[...], wm_ref[:, at], preferred_element_type=f32)
            + jnp.dot(attn_ref[...], wa_ref[:, at], preferred_element_type=f32)
        ).astype(half)

    tiles(width, out_tile)
    sent_a = copies(
        1, lambda p: part_a.at[block(peers[p - 1])], lambda p: got_a.at[p]
    )
    gather_step(0)
    sent_a[0].wait()
    gather_step(1)
    settle(sent_a[1:])
    residual = x_ref[...].astype(f32) + part_a[block(me), :].astype(f32)
    for p in range(1, heads):
        residual = residual + got_a[p].astype(f32)
    d_res_ref[...] = residual
    rms_ffn = lax.rsqrt(jnp.mean(residual * residual, axis=1, keepdims=True) + EPSILON)
    normed_two[block(me), :] = (residual * rms_ffn * gain_two_ref[...]).astype(half)
    sent_n = copies(
        2, lambda p: normed_two.at[block(me)], lambda p: normed_two.at[block(me)]
    )
    gather_step(2)
    settle(sent_n)
    for gather in gathers:
        gather.finish()

    def d_activ_tile(i, carry):
        at = pl.ds(pl.multiple_of(i * tile, tile), tile)
        d_activ[:, at] = dot_back(grad_ref[...], row_tile(down_all, i))
        return carry

    lax.fori_loop(0, units // tile, d_activ_tile, 0)

    for first_unit in range(0, units, tile):
        gate = jnp.dot(
            normed_two[...],
            gu_all[:, :, first_unit : first_unit + tile].reshape(width, tile),
            preferred_element_type=f32,
        )
        up = jnp.dot(
            normed_two[...],
            gu_all[:, :, units + first_unit : units + first_unit + tile].reshape(width, tile),
            preferred_element_type=f32,
        )
        sigmoid = jax.nn.sigmoid(gate)
        silu = gate * sigmoid
        back = d_activ[:, first_unit : first_unit + tile]
        activ[:, first_unit : first_unit + tile] = (silu * up).astype(half)
        d_gate_up[:, first_unit : first_unit + tile] = (
            back * up * (sigmoid * (1.0 + gate * (1.0 - sigmoid)))
        ).astype(half)
        d_gate_up[:, units + first_unit : units + first_unit + tile] = (back * silu).astype(half)

    def d_normed_tile(i, carry):
        at = pl.ds(pl.multiple_of(i * tile, tile), tile)
        part_b[:, at] = dot_back(d_gate_up[...], row_tile(gu_all, i)).astype(half)
        return carry

    lax.fori_loop(0, width // tile, d_normed_tile, 0)
    sent_b = copies(
        3, lambda p: part_b.at[block(peers[p - 1])], lambda p: got_b.at[p]
    )

    def y_tile(at):
        part_c[:, at] = jnp.dot(
            activ[...], down_all[:, :, at].reshape(units, tile), preferred_element_type=f32
        ).astype(half)

    tiles(width, y_tile)

    def gu_grad_tile(at):
        gu_grad_ref[at, :] = dot_rows(normed_two[:, at], d_gate_up[...]).astype(half)

    tiles(width, gu_grad_tile)

    def down_grad_tile(at):
        down_grad_ref[at, :] = dot_rows(activ[:, at], grad_ref[...]).astype(half)

    tiles(units, down_grad_tile)
    gu_work.start(1)
    down_work.start(1)
    gu_work.start(2)

    settle(sent_b)
    residual = d_res_ref[...]
    rms_ffn = lax.rsqrt(jnp.mean(residual * residual, axis=1, keepdims=True) + EPSILON)
    d_normed = part_b[block(me), :].astype(f32)
    for p in range(1, heads):
        d_normed = d_normed + got_b[p].astype(f32)
    scaled = gain_two_ref[...] * d_normed
    d_residual = (
        grad_ref[block(me), :].astype(f32)
        + rms_ffn * scaled
        - residual * (rms_ffn * rms_ffn * rms_ffn)
        * jnp.mean(scaled * residual, axis=1, keepdims=True)
    )
    d_res_all[block(me), :] = d_residual.astype(half)
    sent_d = copies(
        5, lambda p: d_res_all.at[block(me)], lambda p: d_res_all.at[block(me)]
    )
    ffn_gain_grad_ref[...] = jnp.sum(d_normed * residual * rms_ffn, axis=0, keepdims=True)
    sent_c = copies(
        4, lambda p: part_c.at[block(peers[p - 1])], lambda p: got_c.at[p]
    )
    gu_work.pass_on(1)
    down_work.pass_on(1)
    down_work.start(2)
    gu_work.start(3)
    down_work.start(3)
    settle(sent_d)

    d_mixed[...] = dot_back(d_res_all[...], wm_ref[...])
    d_attn_ref[...] = dot_back(d_res_all[...], wa_ref[...]).astype(half)
    pulls[0] = row_totals(gain_mix * d_mixed[...] * gated_ref[...])
    last = copies(6, lambda p: pulls.at[0], lambda p: pulls.at[p])
    gu_work.pass_on(2)
    down_work.pass_on(2)
    gu_work.start(0)
    down_work.start(0)

    def out_grad_tile(at):
        out_grad_ref[pl.ds(0, mine), at] = dot_rows(mixed[...], d_res_all[:, at]).astype(half)
        out_grad_ref[pl.ds(mine, out_grad_ref.shape[0] - mine), at] = dot_rows(
            attn_ref[...], d_res_all[:, at]
        ).astype(half)

    tiles(width, out_grad_tile)
    gu_work.pass_on(3)
    down_work.pass_on(3)
    out_work.start(1)
    out_work.start(2)
    rms_mix = lax.rsqrt(as_column(squares) / dssm + EPSILON)
    mix_gain_grad_ref[...] = jnp.sum(
        d_mixed[...] * gated_ref[...] * rms_mix, axis=0, keepdims=True
    )
    settle(sent_c)
    y_sum = d_res_ref[...] + part_c[block(me), :].astype(f32)
    for p in range(1, heads):
        y_sum = y_sum + got_c[p].astype(f32)
    y_ref[...] = y_sum.astype(half)
    d_res_ref[...] = d_residual
    settle(last)
    pull_mean = as_column(pulls) / dssm
    d_gated_ref[...] = (
        rms_mix * (gain_mix * d_mixed[...])
        - gated_ref[...] * (rms_mix * rms_mix * rms_mix) * pull_mean
    )
    gu_work.pass_on(0)
    down_work.pass_on(0)
    scatter_all([out_work], 2)
    gu_work.finish(gu_sum_ref)
    down_work.finish(down_sum_ref)
    out_work.finish(out_sum_ref)


def middle(heads, gated, attn, out_w, gu, down, x_in, grad_all, gain_mix, gain_two):
    f32 = jnp.float32
    half = jnp.bfloat16
    rows, mine = gated.shape
    tokens, width = x_in.shape
    qcols = attn.shape[1]
    ranges = lax.axis_size("ctx")
    units = down.shape[0] * ranges
    inner = ranges // OUTER
    vmem = pl.BlockSpec(memory_space=pltpu.VMEM)
    out_shape = (
        jax.ShapeDtypeStruct((tokens, width), half),
        jax.ShapeDtypeStruct((tokens, width), f32),
        jax.ShapeDtypeStruct((rows, mine), f32),
        jax.ShapeDtypeStruct((rows, qcols), half),
        jax.ShapeDtypeStruct((units // ranges, width), f32),
        jax.ShapeDtypeStruct((width // ranges, 2 * units), half),
        jax.ShapeDtypeStruct(((mine + qcols) // ranges, width), half),
        jax.ShapeDtypeStruct((1, mine), f32),
        jax.ShapeDtypeStruct((1, width), f32),
    )
    got = pltpu.VMEM((heads, tokens, width), half)
    wide = pltpu.VMEM((rows, width), half)
    return pl.pallas_call(
        functools.partial(middle_kernel, heads),
        out_shape=out_shape,
        in_specs=[vmem] * 9,
        out_specs=[vmem] * len(out_shape),
        scratch_shapes=[
            pltpu.VMEM((heads, 8, rows), f32),
            pltpu.VMEM((heads, 8, rows), f32),
            pltpu.VMEM((rows, mine), half),
            wide,
            got,
            wide,
            pltpu.VMEM((rows, units), f32),
            pltpu.VMEM((rows, units), half),
            pltpu.VMEM((rows, 2 * units), half),
            wide,
            got,
            wide,
            got,
            wide,
            pltpu.VMEM((rows, mine), f32),
            pltpu.VMEM((units, width), half),
            pltpu.VMEM((width, 2 * units), half),
            pltpu.VMEM((mine + qcols, width), half),
            pltpu.VMEM((ranges,) + gu.shape, half),
            pltpu.VMEM((ranges,) + down.shape, half),
            pltpu.SemaphoreType.DMA((7, heads)),
            pltpu.SemaphoreType.DMA((7, heads)),
        ]
        + Scatter.scratch(units // ranges, width, inner)
        + Scatter.scratch(width // ranges, 2 * units, inner)
        + Scatter.scratch((mine + qcols) // ranges, width, inner)
        + LineGather.scratch(2, inner),
        compiler_params=pltpu.CompilerParams(
            collective_id=0, has_side_effects=True, vmem_limit_bytes=56 * MIB
        ),
        cost_estimate=pl.CostEstimate(
            flops=14 * rows * width * units, bytes_accessed=16 * MIB, transcendentals=rows * units
        ),
    )(gated, attn, out_w, gu, down, x_in, grad_all, gain_mix, gain_two)


def on_device(
    x_in,
    in_weight,
    out_weight,
    gu_weight,
    down_weight,
    norm_gain,
    mixer_gain,
    ffn_gain,
    conv_weight,
    conv_bias,
    dt_bias,
    a_log,
    skip_gain,
    out_grad,
):
    f32 = jnp.float32
    half = jnp.bfloat16
    heads = lax.axis_size("head")
    ranges = lax.axis_size("ctx")
    ctx_place = lax.axis_index("ctx")
    head_place = lax.axis_index("head")
    tokens, width = x_in.shape
    rows = tokens * heads
    mix_heads = MH // heads
    attn_heads = AH // heads
    group_devices = heads // KVH
    dssm = MH * MP
    mine = mix_heads * MP
    local_cols = mine + 2 * NS
    qcols = attn_heads * HDIM
    rate_start = 2 * dssm + 2 * NS
    query_start = rate_start + MH
    key_start = query_start + AH * HDIM
    value_start = key_start + KVH * HDIM
    score_scale = 1.0 / math.sqrt(HDIM)
    count = rows // CHUNK
    w_rows = in_weight.shape[0]
    unit_rows = down_weight.shape[0]
    both = ("ctx", "head")

    def columns_for(target):
        kv = target // group_devices
        return jnp.concatenate(
            [
                in_weight[:, target * mine : (target + 1) * mine],
                in_weight[:, dssm + target * mine : dssm + (target + 1) * mine],
                in_weight[:, 2 * dssm : rate_start],
                in_weight[:, query_start + target * qcols : query_start + (target + 1) * qcols],
                in_weight[:, key_start + kv * HDIM : key_start + (kv + 1) * HDIM],
                in_weight[:, value_start + kv * HDIM : value_start + (kv + 1) * HDIM],
                in_weight[:, rate_start + target * mix_heads : rate_start + (target + 1) * mix_heads],
            ],
            axis=1,
        )

    in_cols = jnp.stack([columns_for(target) for target in range(heads)])
    gu_split = gu_weight.reshape(w_rows, 2, ranges, heads, unit_rows)
    gu_cols = gu_split.transpose(3, 0, 1, 2, 4).reshape(heads, w_rows, -1)
    devices = ranges * heads
    rounds = row_matchings(devices, heads)
    here = ctx_place * heads + head_place
    quarter = out_weight.shape[0] // 4
    quarters = out_weight.reshape(4, quarter, width)
    out_rows = jnp.zeros_like(quarters)
    for route, sends, lands in rounds:
        piece = lax.dynamic_index_in_dim(quarters, jnp.asarray(sends)[here], 0, False)
        piece = lax.ppermute(piece, both, route)
        out_rows = lax.dynamic_update_index_in_dim(out_rows, piece, jnp.asarray(lands)[here], 0)
    small = jnp.concatenate(
        [norm_gain, mixer_gain, ffn_gain, conv_weight.reshape(-1), conv_bias]
    )
    small_len = small.size
    small = jnp.pad(small, (0, -small_len % 2048)).reshape(-1, 128)
    in_all, gu_own, small_all, out_all, x_all, grad_all = front(
        heads, in_cols, gu_cols, small, out_rows.reshape(-1, width), x_in, out_grad
    )
    w_in = in_all.reshape(ranges * heads * w_rows, -1)
    w_out = out_all.reshape(-1, width)
    x_all = x_all.reshape(rows, width)
    grad_all = grad_all.reshape(rows, width)
    small_all = small_all.reshape(devices, -1)[:, :small_len]
    units = ranges * unit_rows
    cuts = [0]
    for piece in (norm_gain, mixer_gain, ffn_gain, conv_weight, conv_bias):
        cuts.append(cuts[-1] + piece.size)
    smalls = [small_all[:, cuts[i] : cuts[i + 1]].astype(f32) for i in range(5)]
    gain_one, gain_mix, gain_two = (smalls[i].reshape(-1) for i in range(3))
    conv_w = smalls[3].reshape(-1, KW)
    conv_b = smalls[4].reshape(-1)
    inputs_all = x_all.astype(f32)
    rms_all = lax.rsqrt(jnp.mean(inputs_all * inputs_all, axis=1, keepdims=True) + EPSILON)
    normed = (inputs_all * rms_all * gain_one[None, :]).astype(half)
    proj = jnp.dot(normed, w_in, preferred_element_type=f32).astype(half)
    z_part = proj[:, :mine].astype(f32)
    xbc = proj[:, mine : mine + local_cols]
    at = mine + local_cols
    queries_raw = proj[:, at : at + qcols]
    keys_raw = proj[:, at + qcols : at + qcols + HDIM]
    values_raw = proj[:, at + qcols + HDIM : at + qcols + 2 * HDIM]
    rate_raw = proj[:, at + qcols + 2 * HDIM :]

    query_first = ctx_place * rows
    positions = (query_first + jnp.arange(rows)).astype(f32)
    q_rot = rotate_pairs(
        queries_raw.astype(f32).reshape(rows, attn_heads, HDIM), positions, 1.0
    ).astype(half)
    q_rows = q_rot.transpose(1, 0, 2).reshape(attn_heads * rows, HDIM)
    k_rot = (
        rotate_pairs(keys_raw.astype(f32).reshape(rows, 1, HDIM), positions, 1.0)
        .reshape(rows, HDIM)
        .astype(half)
    )
    kv_own = jnp.concatenate([k_rot, values_raw], axis=1)

    rim = passed_along(xbc[rows - (KW - 1) :], "ctx", 1)
    padded = jnp.concatenate([rim, xbc], axis=0).astype(f32)
    own_w = jnp.concatenate(
        [lax.dynamic_slice_in_dim(conv_w, head_place * mine, mine, 0), conv_w[dssm:]], axis=0
    )
    own_b = jnp.concatenate(
        [lax.dynamic_slice_in_dim(conv_b, head_place * mine, mine, 0), conv_b[dssm:]], axis=0
    )
    conv_pre = jnp.broadcast_to(own_b[None, :], (rows, local_cols))
    for offset in range(KW):
        conv_pre = conv_pre + padded[offset : offset + rows] * own_w[:, offset][None, :]
    conv_out = jax.nn.silu(conv_pre).astype(half)

    def by_chunk(value):
        return value.reshape(count, CHUNK, mix_heads, -1).transpose(0, 2, 1, 3)

    def from_chunk(value):
        return value.transpose(0, 2, 1, 3).reshape(rows, -1)

    mix_x = by_chunk(conv_out[:, :mine])
    bmat = conv_out[:, mine : mine + NS].reshape(count, CHUNK, NS)
    cmat = conv_out[:, mine + NS :].reshape(count, CHUNK, NS)
    dt_pre = (rate_raw.astype(f32) + dt_bias[None, :]).reshape(count, CHUNK, mix_heads)
    dt_pre = dt_pre.transpose(0, 2, 1)
    step = jax.nn.softplus(dt_pre)
    decay_rate = -jnp.exp(a_log)
    lower = jnp.arange(CHUNK)[:, None] >= jnp.arange(CHUNK)[None, :]
    tril = lower.astype(f32)
    cum = jnp.einsum(
        "nhs,ts->nht", step * decay_rate[None, :, None], tril, precision=PRECISE_MODE
    )
    within = jnp.exp(jnp.where(lower, cum[:, :, :, None] - cum[:, :, None, :], -jnp.inf))
    products = ein("ntm,nsm->nts", cmat, bmat)
    mixing = (products[:, None] * within * step[:, :, None, :]).astype(half)
    intra = ein("nhts,nhsp->nhtp", mixing, mix_x)
    x_f = mix_x.astype(f32)
    fade = jnp.exp(cum[:, :, -1:] - cum)
    reach = fade * step
    x_reach = (x_f * reach[..., None]).astype(half)
    ends = ein("nhsp,nsm->nhpm", x_reach, bmat)
    chunk_decay = jnp.exp(cum[:, :, -1])
    range_end = ends[0]
    range_decay = chunk_decay[0]
    for k in range(1, count):
        range_end = chunk_decay[k][:, None, None] * range_end + ends[k]
        range_decay = range_decay * chunk_decay[k]
    decay_rows = jnp.broadcast_to(
        jnp.concatenate([range_decay, jnp.zeros((8 - mix_heads,), f32)])[:, None], (8, NS)
    )
    ends_all, decays_all, kv_all = gather_ctx(
        3, range_end.reshape(mine, NS), decay_rows, kv_own
    )
    gathered = ends_all.reshape(ranges, mix_heads, MP, NS).astype(f32)
    decays = decays_all[:, :mix_heads, 0]

    def weights(order, reached):
        factor = jnp.ones((mix_heads,), f32)
        found = [None] * ranges
        for j in order:
            found[j] = jnp.where(reached(j), factor, 0.0)
            factor = jnp.where(reached(j), factor * decays[j], factor)
        return jnp.stack(found)

    before = weights(range(ranges - 1, -1, -1), lambda j: j < ctx_place)
    after = weights(range(ranges), lambda j: j > ctx_place)
    states = [jnp.sum(before[:, :, None, None] * gathered, axis=0)]
    for k in range(count - 1):
        states.append(chunk_decay[k][:, None, None] * states[k] + ends[k])
    state = jnp.stack(states)
    grown = jnp.exp(cum)
    inter = ein_fine("ntm,nhpm->nhtp", cmat, state) * grown[..., None]
    ssm_full = intra + inter + skip_gain[None, :, None, None] * x_f
    ssm_out = from_chunk(ssm_full.astype(half)).astype(f32)
    gated_mine = ssm_out * jax.nn.silu(z_part)

    causal = jnp.arange(rows)[:, None] >= jnp.arange(rows)[None, :]
    causal = jnp.concatenate([causal] * attn_heads, axis=0)

    def key_block(number):
        piece = lax.dynamic_index_in_dim(kv_all, number, 0, False)
        return (piece[:, :HDIM], piece[:, HDIM:])

    scores = jnp.where(causal, dot_back(q_rows, k_rot) * score_scale, -jnp.inf)
    peak = jnp.max(scores, axis=1, keepdims=True)
    weight = jnp.exp(scores - peak)
    mass = jnp.sum(weight, axis=1, keepdims=True)
    total = jnp.dot(weight.astype(half), values_raw, preferred_element_type=f32)

    def attend(number, carry):
        peak, mass, total = carry
        keys_blk, vals_blk = key_block(number)
        scores = dot_back(q_rows, keys_blk) * score_scale
        new_peak = jnp.maximum(peak, jnp.max(scores, axis=1, keepdims=True))
        weight = jnp.exp(scores - new_peak)
        shrink = jnp.exp(peak - new_peak)
        mass = mass * shrink + jnp.sum(weight, axis=1, keepdims=True)
        total = total * shrink + jnp.dot(
            weight.astype(half), vals_blk, preferred_element_type=f32
        )
        return (new_peak, mass, total)

    peak, mass, total = lax.fori_loop(0, ctx_place, attend, (peak, mass, total))
    log_total = peak + jnp.log(mass)
    attn_rows = (total / mass).astype(half)
    attn_mine = attn_rows.reshape(attn_heads, rows, HDIM).transpose(1, 0, 2).reshape(rows, qcols)

    inputs = x_in.astype(f32)
    rms_in = lax.rsqrt(jnp.mean(inputs * inputs, axis=1, keepdims=True) + EPSILON)
    own_gain = lax.dynamic_slice_in_dim(gain_mix, head_place * mine, mine, 0)
    (
        y_out,
        d_residual,
        d_gated,
        d_attn,
        down_sum,
        gu_sum,
        out_back,
        mix_gain_local,
        ffn_gain_grad,
    ) = middle(
        heads,
        gated_mine,
        attn_mine,
        w_out,
        gu_own.reshape(heads * w_rows, -1),
        down_weight,
        x_in,
        grad_all,
        own_gain[None, :],
        gain_two[None, :],
    )
    out_back = out_back.reshape(4, quarter, width)
    out_sum = jnp.zeros((4, quarter, width), f32)
    for route, sends, lands in rounds:
        piece = lax.dynamic_index_in_dim(out_back, jnp.asarray(lands)[here], 0, False)
        piece = lax.ppermute(piece, both, [(b, a) for a, b in route]).astype(f32)
        out_sum = lax.dynamic_update_index_in_dim(out_sum, piece, jnp.asarray(sends)[here], 0)
    out_sum = out_sum.reshape(-1, width)
    mixer_gain_grad = lax.dynamic_update_slice_in_dim(
        jnp.zeros((dssm,), f32), mix_gain_local[0], head_place * mine, 0
    )
    d_z = d_gated * ssm_out * silu_grad(z_part)
    d_ssm = by_chunk((d_gated * jax.nn.silu(z_part)).astype(half))

    d_grown = (d_ssm.astype(f32) * grown[..., None]).astype(half)
    pulls = ein("nhtp,ntm->nhpm", d_grown, cmat)
    range_pull = pulls[count - 1]
    for k in range(count - 2, -1, -1):
        range_pull = chunk_decay[k][:, None, None] * range_pull + pulls[k]
    (pulls_all,) = gather_ctx(4, range_pull.reshape(mine, NS).astype(half))
    pulls_all = pulls_all.reshape(ranges, mix_heads, MP, NS).astype(f32)
    d_ends = [None] * count
    d_ends[count - 1] = jnp.sum(after[:, :, None, None] * pulls_all, axis=0)
    for k in range(count - 1, 0, -1):
        d_ends[k - 1] = chunk_decay[k][:, None, None] * d_ends[k] + pulls[k]
    d_end = jnp.stack(d_ends)

    d_rows = d_attn.reshape(rows, attn_heads, HDIM).transpose(1, 0, 2)
    d_rows = d_rows.reshape(attn_heads * rows, HDIM)
    row_delta = jnp.sum(d_rows.astype(f32) * attn_rows.astype(f32), axis=1, keepdims=True)

    def back_block(scores, keys_blk, vals_blk):
        probs = jnp.exp(scores - log_total)
        d_probs = dot_back(d_rows, vals_blk)
        d_scores = (probs * (d_probs - row_delta)).astype(half)
        query_part = jnp.dot(d_scores, keys_blk, preferred_element_type=f32)
        key_part = dot_rows(d_scores, q_rows) * score_scale
        value_part = dot_rows(probs.astype(half), d_rows)
        return (query_part, jnp.concatenate([key_part, value_part], axis=1).astype(half))

    own_scores = jnp.where(causal, dot_back(q_rows, k_rot) * score_scale, -jnp.inf)
    query_grad, kv_own_grad = back_block(own_scores, k_rot, values_raw)

    def back_step(number, carry):
        query_grad, kv_grads = carry
        keys_blk, vals_blk = key_block(number)
        query_part, kv_part = back_block(
            dot_back(q_rows, keys_blk) * score_scale, keys_blk, vals_blk
        )
        kv_grads = lax.dynamic_update_index_in_dim(kv_grads, kv_part, number, 0)
        return (query_grad + query_part, kv_grads)

    kv_start = lax.dynamic_update_index_in_dim(
        jnp.zeros((ranges, rows, 2 * HDIM), half), kv_own_grad, ctx_place, 0
    )
    query_grad, kv_grads = lax.fori_loop(0, ctx_place, back_step, (query_grad, kv_start))
    kv_mine = scatter_ctx(5, kv_grads.reshape(ranges * rows, 2 * HDIM), f32)
    query_grad = (query_grad * score_scale).reshape(attn_heads, rows, HDIM).transpose(1, 0, 2)
    d_query = rotate_pairs(query_grad, positions, -1.0).reshape(rows, qcols)
    d_key = rotate_pairs(kv_mine[:, None, :HDIM], positions, -1.0).reshape(rows, HDIM)
    d_value = kv_mine[:, HDIM:]

    d_f = d_ssm.astype(f32)
    overlap = ein("nhtp,nhsp->nhts", d_ssm, mix_x) * within
    weighted = overlap * step[:, :, None, :]
    d_products = jnp.sum(weighted, axis=1)
    felt = overlap * products[:, None]
    felt_sum = jnp.sum(felt, axis=2)
    grad_step = felt_sum
    d_cum = jnp.sum(felt * step[:, :, None, :], axis=3) - step * felt_sum
    grad_b = ein("nts,ntm->nsm", d_products, cmat)
    grad_c = ein("nts,nsm->ntm", d_products, bmat)
    grad_x = ein("nhts,nhtp->nhsp", mixing, d_ssm)
    d_cum = d_cum + jnp.sum(d_f * inter, axis=3)
    grad_c = grad_c + ein_fine("nhtp,nhpm->ntm", d_grown, state)
    d_reach_x = ein("nhpm,nsm->nhsp", d_end, bmat)
    grad_b = grad_b + ein("nhsp,nhpm->nsm", x_reach, d_end)
    grad_x = grad_x + reach[..., None] * d_reach_x + skip_gain[None, :, None, None] * d_f
    d_reach = jnp.sum(d_reach_x * x_f, axis=3)
    grad_step = grad_step + fade * d_reach
    moved = reach * d_reach
    last = jnp.sum(moved, axis=2) + chunk_decay * jnp.sum(d_end * state, axis=(2, 3))
    d_cum = d_cum - moved
    d_rate = jnp.einsum("nht,ts->nhs", d_cum, tril, precision=PRECISE_MODE) + last[:, :, None]
    grad_step = grad_step + d_rate * decay_rate[None, :, None]
    grad_decay = jnp.sum(d_rate * step, axis=(0, 2))
    skip_part = jnp.sum(d_f * x_f, axis=(0, 2, 3))
    d_dt_pre = grad_step * jax.nn.sigmoid(dt_pre)
    head_local = jnp.concatenate(
        [jnp.sum(d_dt_pre, axis=(0, 2)), grad_decay * decay_rate, skip_part]
    )
    d_rates = d_dt_pre.transpose(0, 2, 1).reshape(rows, mix_heads)

    d_conv_pre = jnp.concatenate(
        [from_chunk(grad_x), grad_b.reshape(rows, NS), grad_c.reshape(rows, NS)], axis=1
    ) * silu_grad(conv_pre)
    conv_b_local = jnp.sum(d_conv_pre, axis=0)
    conv_w_local = jnp.stack(
        [jnp.sum(d_conv_pre * padded[offset : offset + rows], axis=0) for offset in range(KW)],
        axis=1,
    )
    edge = passed_along(d_conv_pre[: KW - 1], "ctx", -1)
    d_long = jnp.concatenate([d_conv_pre, edge], axis=0)
    d_xbc = jnp.zeros((rows, local_cols), f32)
    for offset in range(KW):
        shift = KW - 1 - offset
        d_xbc = d_xbc + d_long[shift : shift + rows] * own_w[:, offset][None, :]
    d_proj = jnp.concatenate(
        [d_z, d_xbc, d_query, d_key, d_value, d_rates], axis=1
    ).astype(half)
    d_normed_part = dot_back(d_proj, w_in)
    norm_gain_grad = jnp.sum(d_normed_part * inputs_all * rms_all, axis=0)

    def placed_rows(local):
        full = jnp.zeros((dssm + 2 * NS,) + local.shape[1:], f32)
        full = lax.dynamic_update_slice_in_dim(full, local[:mine], head_place * mine, 0)
        return lax.dynamic_update_slice_in_dim(full, local[mine:], dssm, 0)

    own_head = (jnp.arange(devices) % heads == head_place).astype(f32)
    small_grads = jnp.concatenate(
        [
            norm_gain_grad.reshape(devices, -1),
            mixer_gain_grad.reshape(devices, -1),
            ffn_gain_grad.reshape(devices, -1),
            placed_rows(conv_w_local).reshape(devices, -1),
            placed_rows(conv_b_local).reshape(devices, -1),
            own_head[:, None] * head_local[None, :],
        ],
        axis=1,
    )
    small_count = small_grads.shape[1]
    small_cols = -(-small_count // 1024) * 128
    small_grads = jnp.pad(small_grads, ((0, 0), (0, 8 * small_cols - small_count)))
    in_grad = dot_rows(normed, d_proj).astype(half)
    in_got, small_got, normed_got, gu_got = tail(
        heads,
        in_grad,
        small_grads.reshape(devices * 8, small_cols),
        d_normed_part.astype(half).reshape(heads, tokens, width),
        gu_sum.reshape(heads, w_rows, -1),
    )
    in_got = in_got.astype(f32)
    small_sum = jnp.sum(small_got, axis=0).reshape(-1)[:small_count]
    gu_got = gu_got.astype(f32)
    d_normed = jnp.sum(normed_got.astype(f32), axis=0)
    scaled_in = gain_one[None, :] * d_normed
    x_grad = (
        d_residual
        + rms_in * scaled_in
        - inputs * rms_in**3 * jnp.mean(scaled_in * inputs, axis=1, keepdims=True)
    )

    gate_sum = (
        gu_got.reshape(heads, w_rows, 2, ranges, unit_rows)
        .transpose(1, 2, 3, 0, 4)
        .reshape(w_rows, -1)
    )
    def side_by_side(first, cols):
        return in_got[:, :, first : first + cols].transpose(1, 0, 2).reshape(w_rows, heads * cols)

    def grouped(first):
        piece = in_got[:, :, first : first + HDIM].reshape(KVH, group_devices, w_rows, HDIM)
        return jnp.sum(piece, axis=1).transpose(1, 0, 2).reshape(w_rows, KVH * HDIM)

    input_sum = jnp.concatenate(
        [
            side_by_side(0, mine),
            side_by_side(mine, mine),
            jnp.sum(in_got[:, :, 2 * mine : at], axis=0),
            side_by_side(at + qcols + 2 * HDIM, mix_heads),
            side_by_side(at, qcols),
            grouped(at + qcols),
            grouped(at + qcols + HDIM),
        ],
        axis=1,
    )

    head_sums = small_sum[cuts[5] :].reshape(3, mix_heads)
    return (
        y_out,
        x_grad,
        input_sum,
        out_sum,
        gate_sum,
        down_sum,
        small_sum[cuts[0] : cuts[1]],
        small_sum[cuts[1] : cuts[2]],
        small_sum[cuts[2] : cuts[3]],
        small_sum[cuts[3] : cuts[4]].reshape(-1, KW),
        small_sum[cuts[4] : cuts[5]],
        head_sums[0],
        head_sums[1],
        head_sums[2],
    )


def solution(mesh):
    placed = (
        P(("ctx", "head"), None),
        P(("ctx", "head"), None),
        P(("ctx", "head"), None),
        P(("ctx", "head"), None),
        P(("ctx", "head"), None),
        P(("ctx", "head")),
        P(("ctx", "head")),
        P(("ctx", "head")),
        P(("ctx", "head"), None),
        P(("ctx", "head")),
        P("head"),
        P("head"),
        P("head"),
        P(("ctx", "head"), None),
    )
    return jax.shard_map(
        on_device,
        mesh=mesh,
        in_specs=placed,
        out_specs=(
            P(("ctx", "head"), None),
            P(("ctx", "head"), None),
            P(("ctx", "head"), None),
            P(("ctx", "head"), None),
            P(("ctx", "head"), None),
            P(("ctx", "head"), None),
            P(("ctx", "head")),
            P(("ctx", "head")),
            P(("ctx", "head")),
            P(("ctx", "head"), None),
            P(("ctx", "head")),
            P("head"),
            P("head"),
            P("head"),
        ),
        check_vma=False,
    )
```
